256 devices in a mesh: seq: 64 (over x, z, core), mp: 4 (over y).
Axes of the slice: x: 4, y: 4, z: 8, core: 2. Of those that a mesh axis runs over, the one named last changes fastest.
Arguments:
- voxels: bfloat16 [49152, 1024], P('seq'), may hold values from -6 to 6
- destination: int32 [49152], P('seq'), may hold values from 0 to 98303, as said below
- cond: bfloat16 [4096, 1024], P('seq'), may hold values from -40 to 40
- norm_gain: float32 [1024], replicated, may hold values from 0.1 to 1.9
- qkv_weight: bfloat16 [3, 1024, 1024], P(None, None, 'mp'), may hold values from -0.1875 to 0.1875
- self_out_weight: bfloat16 [1024, 1024], P('mp'), may hold values from -0.1875 to 0.1875
- cross_norm_gain: float32 [1024], replicated, may hold values from 0.1 to 1.9
- cross_q_weight: bfloat16 [1024, 1024], P(None, 'mp'), may hold values from -0.5 to 0.5
- cond_kv_weight: bfloat16 [2, 1024, 1024], P(None, None, 'mp'), may hold values from -0.1875 to 0.1875
- cross_out_weight: bfloat16 [1024, 1024], P('mp'), may hold values from -0.1875 to 0.1875
Outputs:
- layer_out: bfloat16 [49152, 1024], P(('seq', 'mp'))
The draws below stay inside these ranges and needn't reach their ends.
Inputs may be any that keep to these rules, and one draw needn't show every extreme that they name: Write owner = destination // 1536. No two voxels share a destination. Among the rows of one index of seq no owner occurs more than 24 times, on every index some owner occurs exactly 24 times, and some owner occurs 24 times on every index.
All inputs are finite; a program needn't handle non-finite values.
Results may differ from the reference program's by a relative error of at most 0.033.
The reference program's roundings to bfloat16 on the way count: a program that leaves them out, or rounds other values in their place, can miss the bound.
Values may be sent and summed in bfloat16 or wider, within the bound.
A program may use at most 64 MiB of HBM per device.

```python
import jax
import jax.numpy as jnp
from jax import lax

D = 1024
HEADS = 16
HD = 64
DC = 1024
COND = 4096
WBLK = 64
VOX_DEV = 768
VOX = 49152
SLOTS = 1536
N_SEQ = 64


def draw_cond(key, part):
    values = jax.random.normal(jax.random.fold_in(key, 11), (COND, DC), jnp.float32)
    return jnp.clip(values, -40.0, 40.0).astype(jnp.bfloat16)


def draw_destination(key, part):
    base = jax.random.fold_in(key, 101)
    slot_total = 2 * VOX_DEV
    capacity = slot_total // N_SEQ
    position = jnp.arange(slot_total, dtype=jnp.int32)

    def owner_order(order_key):
        return jax.random.randint(order_key, (slot_total,), 0, 4096, dtype=jnp.int32)

    def shuffle_rows(row_key):
        return jax.random.permutation(row_key, VOX_DEV).astype(jnp.int32)
    order_keys = jax.random.split(jax.random.fold_in(base, 1), N_SEQ)
    order_scores = jax.vmap(owner_order)(order_keys) * slot_total + position[None, :]
    order_scores = order_scores.at[:, 0].set(-2).at[:, slot_total - 1].set(-1)
    orders = jnp.argsort(order_scores, axis=1, stable=True).astype(jnp.int32)
    groups = orders.reshape(N_SEQ, N_SEQ, capacity)
    shift = jax.random.randint(jax.random.fold_in(base, 2), (), 0, N_SEQ, dtype=jnp.int32)
    hot_owner = jax.random.randint(jax.random.fold_in(base, 3), (), 0, N_SEQ, dtype=jnp.int32)
    indices = jnp.arange(N_SEQ, dtype=jnp.int32)
    group_index = (indices[None, :] - indices[:, None] + shift) % N_SEQ
    reserved = jnp.take_along_axis(groups, jnp.broadcast_to(group_index[:, :, None], (N_SEQ, N_SEQ, capacity)), axis=1)
    reserved = jnp.transpose(reserved, (1, 0, 2)).reshape(N_SEQ, slot_total)
    forced_owner = (indices + shift) % N_SEQ
    forced = jnp.where(indices[None, :] == forced_owner[:, None], 32768, 0).astype(jnp.int32)
    forced = forced + jnp.where(indices == hot_owner, 16384, 0).astype(jnp.int32)[None, :]
    bias = jax.random.randint(jax.random.fold_in(base, 4), (N_SEQ,), 0, 6144, dtype=jnp.int32)
    noise = jax.random.randint(jax.random.fold_in(base, 5), (N_SEQ, N_SEQ, capacity), 0, 4096, dtype=jnp.int32)
    scores = noise + (bias[None, :] + forced)[:, :, None]
    ranked = scores.reshape(N_SEQ, slot_total) * slot_total + position[None, :]
    chosen = lax.top_k(ranked, VOX_DEV)[1].astype(jnp.int32)
    owners = chosen // capacity
    slot_ids = jnp.take_along_axis(reserved, chosen, axis=1)
    row_keys = jax.random.split(jax.random.fold_in(base, 6), N_SEQ)
    shuffles = jax.vmap(shuffle_rows)(row_keys)
    owners = jnp.take_along_axis(owners, shuffles, axis=1)
    slot_ids = jnp.take_along_axis(slot_ids, shuffles, axis=1)
    return (owners * slot_total + slot_ids).reshape(N_SEQ * VOX_DEV).astype(jnp.int32)


def level_of(stream_key, shape, cuts, smallest, top_value):
    level = 1.0
    for axis_at, parts in cuts:
        heights = jax.random.uniform(jax.random.fold_in(jax.random.fold_in(stream_key, 6), axis_at), (parts,), jnp.float32, smallest / len(cuts), top_value / len(cuts))
        level = level * jnp.repeat(jnp.exp(heights), shape[axis_at] // parts).reshape((-1,) + (1,) * (len(shape) - 1 - axis_at))
    return level


def normal_values(stream_key, shape, scale, reach, shards=(), kind=jnp.bfloat16):
    result = scale * jax.random.normal(stream_key, shape, jnp.float32)
    if shards:
        result = result * level_of(stream_key, shape, shards, -0.22, 0.18)
    return jnp.clip(result, -reach, reach).astype(kind)


def setup_inputs(seed: int = 0) -> dict:
    streams_of = jax.random.split(jax.random.key(seed), 11)
    voxels = normal_values(streams_of[0], (VOX, D), 1.0, 6.0, ((0, 64),))
    destination = draw_destination(jax.random.fold_in(streams_of[10], 71), 0)
    cond = draw_cond(jax.random.fold_in(streams_of[10], 71), 0)
    norm_gain = jnp.clip(1.0 + 0.18 * jax.random.normal(streams_of[3], (D,), jnp.float32), 0.1, 1.9)
    qkv_weight = normal_values(streams_of[4], (3, D, D), D ** -0.5, 0.1875, ((2, 4),))
    self_out_weight = normal_values(streams_of[5], (D, D), D ** -0.5, 0.1875, ((0, 4),))
    cross_norm_gain = jnp.clip(1.0 + 0.18 * jax.random.normal(streams_of[6], (D,), jnp.float32), 0.1, 1.9)
    cross_q_weight = normal_values(streams_of[7], (D, D), (D // 9) ** -0.5, 0.5, ((1, 4),))
    cond_kv_weight = normal_values(streams_of[8], (2, DC, D), DC ** -0.5, 0.1875, ((2, 4),))
    cross_out_weight = normal_values(streams_of[9], (D, D), D ** -0.5, 0.1875, ((0, 4),))
    return dict(voxels=voxels, destination=destination, cond=cond, norm_gain=norm_gain, qkv_weight=qkv_weight, self_out_weight=self_out_weight, cross_norm_gain=cross_norm_gain, cross_q_weight=cross_q_weight, cond_kv_weight=cond_kv_weight, cross_out_weight=cross_out_weight)


def rms_norm(matrix, gain):
    values = matrix.astype(jnp.float32)
    spread = lax.optimization_barrier(jnp.mean(values * values, axis=-1, keepdims=True))
    return (values * lax.rsqrt(spread + 1e-06) * gain).astype(jnp.bfloat16)

def window_block(queries, keyset, valset, occupied, head_count):
    window_count = queries.shape[0] // WBLK
    query_heads = queries.astype(jnp.float32).reshape(window_count, WBLK, head_count, HD)
    key_heads = keyset.astype(jnp.float32).reshape(window_count, WBLK, head_count, HD)
    value_heads = valset.astype(jnp.float32).reshape(window_count, WBLK, head_count, HD)
    scores = jnp.einsum('wqhd,wkhd->whqk', query_heads, key_heads) * HD ** (-0.5)
    diagonal = jnp.arange(WBLK, dtype=jnp.int32)[:, None] == jnp.arange(WBLK, dtype=jnp.int32)[None, :]
    allowed = occupied.reshape(window_count, 1, WBLK) | diagonal[None]
    weights = jnp.where(allowed[:, None], jnp.exp(scores), 0.0)
    totals = lax.optimization_barrier(jnp.sum(weights, axis=-1))
    mixed = jnp.einsum('whqk,wkhd->wqhd', weights.astype(jnp.bfloat16).astype(jnp.float32), value_heads)
    mixed = mixed / jnp.transpose(totals, (0, 2, 1))[:, :, :, None]
    return mixed.astype(jnp.bfloat16).reshape(window_count * WBLK, head_count * HD)

def attend_block(query_block, key_rows, value_rows, head_count):
    queries = query_block.astype(jnp.float32).reshape(query_block.shape[0], head_count, HD)
    keyset = key_rows.astype(jnp.float32).reshape(key_rows.shape[0], head_count, HD)
    valset = value_rows.astype(jnp.float32).reshape(value_rows.shape[0], head_count, HD)
    scores = jnp.einsum('qhd,khd->hqk', queries, keyset) * HD ** (-0.5)
    row_max = lax.optimization_barrier(jnp.max(scores, axis=-1, keepdims=True))
    weights = jnp.exp(scores - row_max)
    totals = lax.optimization_barrier(jnp.sum(weights, axis=-1))
    mixed = jnp.einsum('hqk,khd->qhd', weights.astype(jnp.bfloat16).astype(jnp.float32), valset)
    mixed = mixed / jnp.transpose(totals)[:, :, None]
    return mixed.astype(jnp.bfloat16).reshape(query_block.shape[0], head_count * HD)

def reference(voxels, destination, cond, norm_gain, qkv_weight, self_out_weight, cross_norm_gain, cross_q_weight, cond_kv_weight, cross_out_weight):
    normed = rms_norm(voxels, norm_gain)
    projected = [jnp.dot(normed, qkv_weight[index], preferred_element_type=jnp.float32).astype(jnp.bfloat16) for index in range(3)]
    total_slots = N_SEQ * SLOTS
    layouts = [jnp.zeros((total_slots, D), jnp.bfloat16).at[destination].set(item).reshape(N_SEQ, SLOTS, D) for item in projected]
    occupied = jnp.zeros((total_slots,), jnp.bool_).at[destination].set(True).reshape(N_SEQ, SLOTS)

    def attend_owner(operands):
        return window_block(operands[0], operands[1], operands[2], operands[3], HEADS)
    mixed = lax.map(attend_owner, (layouts[0], layouts[1], layouts[2], occupied))
    window_mix = mixed.reshape(total_slots, D)[destination]
    hidden = voxels.astype(jnp.float32) + jnp.dot(window_mix, self_out_weight, preferred_element_type=jnp.float32)
    normed2 = rms_norm(hidden, cross_norm_gain)
    cross_query = jnp.dot(normed2, cross_q_weight, preferred_element_type=jnp.float32).astype(jnp.bfloat16)
    cond_key = jnp.dot(cond, cond_kv_weight[0], preferred_element_type=jnp.float32).astype(jnp.bfloat16)
    cond_value = jnp.dot(cond, cond_kv_weight[1], preferred_element_type=jnp.float32).astype(jnp.bfloat16)
    block_size = min(512, VOX)

    def cross_inner(query_block):
        return attend_block(query_block, cond_key, cond_value, HEADS)
    cross_mix = lax.map(cross_inner, cross_query.reshape(VOX // block_size, block_size, D)).reshape(VOX, D)
    layer_out = hidden + jnp.dot(cross_mix, cross_out_weight, preferred_element_type=jnp.float32)
    return layer_out.astype(jnp.bfloat16)
```

```python
import functools

import jax
import jax.numpy as jnp
from jax import lax
from jax.experimental import pallas as pl
from jax.experimental.pallas import tpu as pltpu
from jax.sharding import PartitionSpec as P

F32 = jnp.float32
BF16 = jnp.bfloat16
I32 = jnp.int32
MESH = pl.DeviceIdType.MESH

ROWS = 768
D = 1024
W = 256
HD = 64
WBLK = 64
CAP = 24
PEERS = 64
SLOTS = PEERS * CAP
GROUP = 8
NG = PEERS // GROUP
TOKENS = 4096
SHARE = ROWS // 4


def dot(a, b, ca, cb):
    return lax.dot_general(a, b, (((ca,), (cb,)), ((), ())), preferred_element_type=F32)


def iota(shape, axis):
    return lax.broadcasted_iota(I32, shape, axis)


def offset_of(k):
    dc = 1 - (k & 1)
    a = (k >> 1) & 7
    b = k >> 4
    half_a = (a + 1) >> 1
    dz = (4 + (a >> 1)) * (1 - (a & 1)) + (4 - half_a) * (a & 1)
    dx = (2 + (b >> 1)) * (1 - (b & 1)) + (2 - ((b + 1) >> 1)) * (b & 1)
    return dx & 3, dz & 7, dc


def partner(me, k, sign):
    dx, dz, dc = offset_of(k)
    x, z, c = me >> 4, (me >> 1) & 7, me & 1
    return (((x + sign * dx) & 3) << 4) | (((z + sign * dz) & 7) << 1) | ((c + dc) & 1)


def whole(n):
    return [pl.BlockSpec(memory_space=pltpu.VMEM)] * n


def to_chunks(rows):
    cut = rows.reshape(PEERS, CAP, W)
    return jnp.concatenate([cut[:, :, :128], cut[:, :, 128:]], axis=1).astype(BF16)


def half_of(chunks, half):
    wide = chunks.astype(F32)[:, half * CAP : (half + 1) * CAP, :]
    return wide.reshape(SLOTS, 128).astype(BF16)


def pack_kernel(vox_ref, dest_ref, gain_ref, s_ref, m_ref, col_ref):
    me = lax.axis_index("seq")
    plane = lax.axis_index("mp")
    vox = vox_ref[...].astype(F32)
    spread = jnp.mean(vox * vox, axis=-1, keepdims=True)
    cols = pl.ds(pl.multiple_of(plane * W, W), W)
    normed = (vox_ref[:, cols].astype(F32) * lax.rsqrt(spread + 1e-06) * gain_ref[:, cols]).astype(BF16)
    dest = dest_ref[...]
    peer = partner(me, iota((PEERS, 1), 0), 1)
    low = peer * SLOTS
    match = (dest >= low) & (dest < low + SLOTS)
    matchf = jnp.where(match, 1.0, 0.0)
    upper = jnp.where(iota((ROWS, ROWS), 0) <= iota((ROWS, ROWS), 1), 1.0, 0.0).astype(BF16)
    count = dot(matchf.astype(BF16), upper, 1, 0)
    within = jnp.sum(matchf * count, axis=0, keepdims=True) - 1.0
    kk = jnp.sum(matchf * iota((PEERS, 1), 0).astype(F32), axis=0, keepdims=True)
    slot = jnp.sum(jnp.where(match, dest - low, 0), axis=0, keepdims=True)
    high = ((slot >> 6) + 1).astype(F32)
    rest = (slot & 63).astype(F32)
    cap_hot = jnp.where(within == iota((128, 1), 0).astype(F32), 1.0, 0.0).astype(BF16)
    mh = dot((matchf * high).astype(BF16), cap_hot, 1, 1)
    ml = dot((matchf * rest).astype(BF16), cap_hot, 1, 1)
    places = (mh * 64.0 + ml).astype(I32) - 64
    for k in range(PEERS):
        m_ref[k] = places[k : k + 1, :]
    sent = (kk * CAP + within).astype(I32)
    hot = jnp.where(iota((SLOTS, 1), 0) == sent, 1.0, 0.0).astype(BF16)
    s_ref[...] = to_chunks(dot(hot, normed, 1, 0))
    eye = jnp.where(iota((ROWS, ROWS), 0) == iota((ROWS, ROWS), 1), 1.0, 0.0).astype(BF16)
    ck = dot(eye, jnp.broadcast_to(kk, (8, ROWS)).astype(BF16), 1, 1)
    cw = dot(eye, jnp.broadcast_to(within, (8, ROWS)).astype(BF16), 1, 1)
    col_ref[...] = (ck * CAP + cw).astype(I32)[:, :1]


def pack(voxels, destination, gain):
    return pl.pallas_call(
        pack_kernel,
        out_shape=(
            jax.ShapeDtypeStruct((PEERS, 2 * CAP, 128), BF16),
            jax.ShapeDtypeStruct((PEERS, 1, 128), I32),
            jax.ShapeDtypeStruct((ROWS, 1), I32),
        ),
        in_specs=whole(3),
        out_specs=tuple(whole(3)),
        name="pack",
    )(voxels, destination.reshape(1, ROWS), gain.reshape(1, D))


def out_kernel(s_ref, m_ref, r_ref, mo_ref, send, msend, ysend, own_sem, recv, mrecv, above, below, far):
    me = lax.axis_index("seq")
    plane = lax.axis_index("mp")
    up, down = (plane + 1) & 3, (plane + 3) & 3
    across = (plane + 2) & 3
    barrier = pltpu.get_barrier_semaphore()

    @pl.loop(0, PEERS - 1)
    def _(k):
        pl.semaphore_signal(barrier, inc=1, device_id={"seq": partner(me, k, 1)}, device_id_type=MESH)

    for y in (up, down):
        pl.semaphore_signal(barrier, inc=1, device_id={"mp": y}, device_id_type=MESH)
    pl.semaphore_wait(barrier, PEERS + 1)
    own_copy = pltpu.make_async_copy(s_ref.at[PEERS - 1], r_ref.at[plane, PEERS - 1], own_sem.at[0])
    own_copy.start()
    own_meta = pltpu.make_async_copy(m_ref.at[PEERS - 1], mo_ref.at[PEERS - 1], own_sem.at[1])
    own_meta.start()

    @pl.loop(0, PEERS - 1)
    def _(k):
        to = {"seq": partner(me, k, 1)}
        pltpu.make_async_remote_copy(
            s_ref.at[k], r_ref.at[plane, k], send, recv.at[k >> 3], device_id=to, device_id_type=MESH
        ).start()
        pltpu.make_async_remote_copy(
            m_ref.at[k], mo_ref.at[k], msend, mrecv, device_id=to, device_id_type=MESH
        ).start()

    own_copy.wait()
    own_meta.wait()

    def piece(y, g, n=GROUP):
        return r_ref.at[y, pl.ds(g * GROUP, n)]

    def relay(y_piece, g, sem, to):
        return pltpu.make_async_remote_copy(
            piece(y_piece, g), piece(y_piece, g), ysend, sem, device_id={"mp": to}, device_id_type=MESH
        )

    def first(g, n):
        pltpu.make_async_copy(piece(plane, g, n), piece(plane, g, n), recv.at[g]).wait()
        relay(plane, g, above.at[g], down).start()
        relay(plane, g, below.at[g], up).start()

    def second(g):
        pltpu.make_async_copy(piece(down, g), piece(down, g), below.at[g]).wait()
        pltpu.make_async_copy(piece(up, g), piece(up, g), above.at[g]).wait()
        odd = g & 1
        relay((down + 2 * odd) & 3, g, far.at[g], (up + 2 * odd) & 3).start()

    first(0, GROUP)

    @pl.loop(1, NG - 1)
    def _(g):
        first(g, GROUP)
        second(g - 1)

    first(NG - 1, GROUP - 1)
    second(NG - 2)
    second(NG - 1)

    @pl.loop(0, NG)
    def _(g):
        pltpu.make_async_copy(piece(across, g), piece(across, g), far.at[g]).wait()

    most = pl.ds(0, PEERS - 1)
    pltpu.make_async_copy(mo_ref.at[most], mo_ref.at[most], mrecv).wait()
    pltpu.make_async_copy(s_ref.at[most], s_ref.at[most], send).wait()
    pltpu.make_async_copy(m_ref.at[most], m_ref.at[most], msend).wait()
    three = r_ref.at[pl.ds(0, 3)]
    pltpu.make_async_copy(three, three, ysend).wait()


def send_out(chunks, meta):
    return pl.pallas_call(
        out_kernel,
        out_shape=(
            jax.ShapeDtypeStruct((4, PEERS, 2 * CAP, 128), BF16),
            jax.ShapeDtypeStruct((PEERS, 1, 128), I32),
        ),
        in_specs=whole(2),
        out_specs=tuple(whole(2)),
        scratch_shapes=[
            pltpu.SemaphoreType.DMA,
            pltpu.SemaphoreType.DMA,
            pltpu.SemaphoreType.DMA,
            pltpu.SemaphoreType.DMA((2,)),
            pltpu.SemaphoreType.DMA((NG,)),
            pltpu.SemaphoreType.DMA,
            pltpu.SemaphoreType.DMA((NG,)),
            pltpu.SemaphoreType.DMA((NG,)),
            pltpu.SemaphoreType.DMA((NG,)),
        ],
        compiler_params=pltpu.CompilerParams(collective_id=0, has_side_effects=True),
        name="send_out",
    )(chunks, meta)


def window_kernel(r_ref, m_ref, w_ref, o_ref, x_ref, pr_ref, qkv_ref, pt_ref, p_ref, mix_ref):
    places = m_ref[...].reshape(PEERS, 128)
    lane = iota((PEERS, CAP, 128), 2) == iota((PEERS, CAP, 128), 1)
    col = jnp.sum(jnp.where(lane, places.reshape(PEERS, 1, 128), 0), axis=2, keepdims=True).reshape(SLOTS, 1)
    pt_ref[...] = jnp.where(col == iota((1, SLOTS), 1), 1.0, 0.0).astype(BF16)
    code = places + 64
    k_hot = jnp.where(
        (iota((PEERS, SLOTS), 1) >= iota((PEERS, SLOTS), 0) * CAP)
        & (iota((PEERS, SLOTS), 1) < iota((PEERS, SLOTS), 0) * CAP + CAP),
        1.0,
        0.0,
    ).astype(BF16)
    th = dot((code >> 6).astype(F32).astype(BF16), k_hot, 0, 0)
    tl = dot((code & 63).astype(F32).astype(BF16), k_hot, 0, 0)
    pos = iota((1, SLOTS), 1).astype(F32)
    pos = pos - CAP * jnp.floor((pos + 0.5) * (1.0 / CAP))
    row = jnp.sum(
        jnp.where(iota((128, 1), 0).astype(F32) == pos, th * 64.0 + tl, 0.0), axis=0, keepdims=True
    ).astype(I32) - 64

    @pl.loop(0, SLOTS // 256)
    def _(i):
        r = pl.ds(pl.multiple_of(i * 256, 256), 256)
        p_ref[r, :] = jnp.where(iota((256, 1), 0) + i * 256 == row, 1.0, 0.0).astype(BF16)

    for y in range(4):
        for half in range(2):
            at = y * W + half * 128
            x_ref[:, at : at + 128] = half_of(r_ref[y], half)

    @pl.loop(0, SLOTS // 256)
    def _(i):
        r = pl.ds(pl.multiple_of(i * 256, 256), 256)
        for c in range(3):
            pr_ref[r, c * W : (c + 1) * W] = dot(x_ref[r, :], w_ref[c], 1, 0).astype(BF16)

    occupied = dot(jnp.full((8, SLOTS), 1.0, BF16), pt_ref[...], 1, 0)
    same = (iota((256, 256), 0) >> 6) == (iota((256, 256), 1) >> 6)
    head = iota((1, W), 1) >> 6

    @pl.loop(0, SLOTS // 256)
    def _(i):
        r = pl.ds(pl.multiple_of(i * 256, 256), 256)
        qkv_ref[r, :] = dot(p_ref[r, :], pr_ref[...], 1, 0).astype(BF16)

    for i in range(SLOTS // 256):
        r = slice(i * 256, (i + 1) * 256)
        q = qkv_ref[r, 0:W]
        k = qkv_ref[r, W : 2 * W]
        v = qkv_ref[r, 2 * W : 3 * W]
        mask = same & (occupied[:1, i * 256 : (i + 1) * 256] > 0.5)
        out = jnp.zeros((256, W), F32)
        for h in range(4):
            scores = dot(jnp.where(head == h, q, 0), k, 1, 1) * HD ** (-0.5)
            weights = jnp.where(mask, jnp.exp(scores), 0.0)
            totals = jnp.sum(weights, axis=-1, keepdims=True)
            totals = jnp.where(totals == 0.0, 1.0, totals)
            mixed = dot(weights.astype(BF16), v, 1, 0)
            out = jnp.where(head == h, mixed / totals, out)
        mix_ref[r, :] = out.astype(BF16)

    o_ref[...] = to_chunks(dot(pt_ref[...], mix_ref[...], 1, 0))


def window(received, meta, qkv_weight):
    return pl.pallas_call(
        window_kernel,
        out_shape=jax.ShapeDtypeStruct((PEERS, 2 * CAP, 128), BF16),
        in_specs=whole(3),
        out_specs=whole(1)[0],
        scratch_shapes=[
            pltpu.VMEM((SLOTS, D), BF16),
            pltpu.VMEM((SLOTS, 3 * W), BF16),
            pltpu.VMEM((SLOTS, 3 * W), BF16),
            pltpu.VMEM((SLOTS, SLOTS), BF16),
            pltpu.VMEM((SLOTS, SLOTS), BF16),
            pltpu.VMEM((SLOTS, W), BF16),
        ],
        name="window",
    )(received, meta, qkv_weight)


def back_kernel(s_ref, r_ref, send, recv, own_sem):
    me = lax.axis_index("seq")
    barrier = pltpu.get_barrier_semaphore()

    @pl.loop(0, PEERS - 1)
    def _(k):
        pl.semaphore_signal(barrier, inc=1, device_id={"seq": partner(me, k, -1)}, device_id_type=MESH)

    pl.semaphore_wait(barrier, PEERS - 1)
    own_copy = pltpu.make_async_copy(s_ref.at[PEERS - 1], r_ref.at[PEERS - 1], own_sem)
    own_copy.start()

    @pl.loop(0, PEERS - 1)
    def _(k):
        pltpu.make_async_remote_copy(
            s_ref.at[k], r_ref.at[k], send, recv, device_id={"seq": partner(me, k, -1)}, device_id_type=MESH
        ).start()

    own_copy.wait()
    most = pl.ds(0, PEERS - 1)
    pltpu.make_async_copy(r_ref.at[most], r_ref.at[most], recv).wait()
    pltpu.make_async_copy(s_ref.at[most], s_ref.at[most], send).wait()


def send_back(chunks):
    return pl.pallas_call(
        back_kernel,
        out_shape=jax.ShapeDtypeStruct((PEERS, 2 * CAP, 128), BF16),
        in_specs=whole(1),
        out_specs=whole(1)[0],
        scratch_shapes=[pltpu.SemaphoreType.DMA, pltpu.SemaphoreType.DMA, pltpu.SemaphoreType.DMA],
        compiler_params=pltpu.CompilerParams(collective_id=1, has_side_effects=True),
        name="send_back",
    )(chunks)


def rows_kernel(b_ref, col_ref, o_ref):
    hot = jnp.where(col_ref[...] == iota((1, SLOTS), 1), 1.0, 0.0).astype(BF16)
    back = jnp.concatenate([half_of(b_ref[...], 0), half_of(b_ref[...], 1)], axis=1)
    o_ref[...] = dot(hot, back, 1, 0).astype(BF16)


def rows_of(back, col):
    return pl.pallas_call(
        rows_kernel,
        out_shape=jax.ShapeDtypeStruct((ROWS, W), BF16),
        in_specs=whole(2),
        out_specs=whole(1)[0],
        name="rows",
    )(back, col)


def swap_kernel(s_ref, r_ref, send, recv, own_sem):
    plane = lax.axis_index("mp")
    barrier = pltpu.get_barrier_semaphore()
    for step in (2, 1, 3):
        pl.semaphore_signal(barrier, inc=1, device_id={"mp": (plane + step) & 3}, device_id_type=MESH)
    pl.semaphore_wait(barrier, 3)
    copies = []
    for step in (2, 1, 3):
        to = (plane + step) & 3
        copy = pltpu.make_async_remote_copy(
            s_ref.at[to], r_ref.at[plane], send.at[step], recv.at[step], device_id={"mp": to}, device_id_type=MESH
        )
        copy.start()
        copies.append(copy)
    own_copy = pltpu.make_async_copy(s_ref.at[plane], r_ref.at[plane], own_sem)
    own_copy.start()
    own_copy.wait()
    for copy in copies:
        copy.wait()


def swap(blocks, cid):
    return pl.pallas_call(
        swap_kernel,
        out_shape=jax.ShapeDtypeStruct(blocks.shape, blocks.dtype),
        in_specs=whole(1),
        out_specs=whole(1)[0],
        scratch_shapes=[pltpu.SemaphoreType.DMA((4,)), pltpu.SemaphoreType.DMA((4,)), pltpu.SemaphoreType.DMA],
        compiler_params=pltpu.CompilerParams(collective_id=cid, has_side_effects=True),
        name="swap",
    )(blocks)


def hidden_kernel(vox_ref, mix_ref, wo_ref, gain_ref, wq_ref, hid_ref, q_ref):
    plane = lax.axis_index("mp")
    rows = pl.ds(pl.multiple_of(plane * SHARE, SHARE), SHARE)
    mix = jnp.concatenate([mix_ref[y] for y in range(4)], axis=1)
    hidden = vox_ref[rows, :].astype(F32) + dot(mix, wo_ref[...], 1, 0)
    hid_ref[...] = hidden
    spread = jnp.mean(hidden * hidden, axis=-1, keepdims=True)
    normed = (hidden * lax.rsqrt(spread + 1e-06) * gain_ref[...]).astype(BF16)
    for y in range(4):
        q_ref[y] = dot(normed, wq_ref[y], 1, 0).astype(BF16)


def hidden_of(voxels, mix, wo, gain, wq):
    return pl.pallas_call(
        hidden_kernel,
        out_shape=(jax.ShapeDtypeStruct((SHARE, D), F32), jax.ShapeDtypeStruct((4, SHARE, W), BF16)),
        in_specs=whole(5),
        out_specs=tuple(whole(2)),
        name="hidden",
    )(voxels, mix, wo, gain.reshape(1, D), wq)


QB = 256
KB = 1024


def cross_kernel(q_ref, kv_ref, o_ref, s_ref):
    head = iota((1, W), 1) >> 6

    @pl.loop(0, ROWS // QB)
    def _(i):
        r = pl.ds(pl.multiple_of(i * QB, QB), QB)
        q = q_ref[r, :] * BF16(HD ** (-0.5))
        out = jnp.zeros((QB, W), F32)
        for h in range(4):
            qh = jnp.where(head == h, q, BF16(0))
            top = jnp.full((QB, 128), -jnp.inf, F32)
            for b in range(TOKENS // KB):
                s = dot(qh, kv_ref[b * KB : (b + 1) * KB, 0:W], 1, 1)
                s_ref[:, b * KB : (b + 1) * KB] = s
                for c in range(KB // 128):
                    top = jnp.maximum(top, s[:, c * 128 : (c + 1) * 128])
            top = jnp.max(top, axis=-1, keepdims=True)
            total = jnp.zeros((QB, 128), F32)
            mixed = jnp.zeros((QB, W), F32)
            for b in range(TOKENS // KB):
                e = jnp.exp(s_ref[:, b * KB : (b + 1) * KB] - top)
                for c in range(KB // 128):
                    total = total + e[:, c * 128 : (c + 1) * 128]
                mixed = mixed + dot(e.astype(BF16), kv_ref[b * KB : (b + 1) * KB, W : 2 * W], 1, 0)
            total = jnp.sum(total, axis=-1, keepdims=True)
            out = jnp.where(head == h, mixed / total, out)
        o_ref[r, :] = out.astype(BF16)


def cross(query, kv):
    return pl.pallas_call(
        cross_kernel,
        out_shape=jax.ShapeDtypeStruct((ROWS, W), BF16),
        in_specs=whole(2),
        out_specs=whole(1)[0],
        scratch_shapes=[pltpu.VMEM((QB, TOKENS), F32)],
        name="cross",
    )(query, kv)


def final_kernel(hid_ref, mix_ref, wo_ref, o_ref):
    mix = jnp.concatenate([mix_ref[y] for y in range(4)], axis=1)
    o_ref[...] = (hid_ref[...] + dot(mix, wo_ref[...], 1, 0)).astype(BF16)


def final(hidden, mix, wo):
    return pl.pallas_call(
        final_kernel,
        out_shape=jax.ShapeDtypeStruct((SHARE, D), BF16),
        in_specs=whole(3),
        out_specs=whole(1)[0],
        name="final",
    )(hidden, mix, wo)


def shards(voxels, destination, cond, norm_gain, qkv_weight, self_out_weight, cross_norm_gain, cross_q_weight, cond_kv_weight, cross_out_weight):
    kv = jnp.concatenate(
        [jnp.dot(cond, cond_kv_weight[i], preferred_element_type=F32).astype(BF16) for i in range(2)], axis=1
    )
    kv = lax.all_gather(kv, "seq", axis=0, tiled=True)
    wo1 = lax.all_gather(self_out_weight, "mp", axis=0, tiled=True)
    wq = lax.all_gather(cross_q_weight, "mp", axis=0)
    wo2 = lax.all_gather(cross_out_weight, "mp", axis=0, tiled=True)
    chunks, meta, col = pack(voxels, destination, norm_gain)
    received, places = send_out(chunks, meta)
    mixed = window(received, places, qkv_weight)
    window_mix = rows_of(send_back(mixed), col)
    mine = swap(window_mix.reshape(4, SHARE, W), 2)
    hidden, query = hidden_of(voxels, mine, wo1, cross_norm_gain, wq)
    query = swap(query, 3).reshape(ROWS, W)
    cross_mix = swap(cross(query, kv).reshape(4, SHARE, W), 4)
    return final(hidden, cross_mix, wo2)


def solution(mesh):
    return jax.shard_map(
        shards,
        mesh=mesh,
        in_specs=(
            P("seq", None),
            P("seq"),
            P("seq", None),
            P(),
            P(None, None, "mp"),
            P("mp", None),
            P(),
            P(None, "mp"),
            P(None, None, "mp"),
            P("mp", None),
        ),
        out_specs=P(("seq", "mp"), None),
        check_vma=False,
    )
```
